32 devices in a mesh: row: 8 (over z, core), col: 4 (over y, x).
Axes of the slice: x: 2, y: 2, z: 4, core: 2. Of those that a mesh axis runs over, the one named last changes fastest.
Arguments:
- alignment: bfloat16 [256, 16384], P('row', 'col'), may hold values from -6 to 6
- pair_state: float32 [256, 256, 128], P('row', 'col'), may hold values from -6 to 6
- alignment_factor_weight: bfloat16 [64, 64], replicated, may hold values from -0.75 to 0.75
- outer_proj: bfloat16 [1024, 128], replicated, may hold values from -3 to 3
- outgoing_proj: bfloat16 [128, 640], replicated, may hold values from -0.5 to 0.5
- outgoing_final: bfloat16 [128, 128], replicated, may hold values from -0.5 to 0.5
- incoming_proj: bfloat16 [128, 640], replicated, may hold values from -0.5 to 0.5
- incoming_final: bfloat16 [128, 128], replicated, may hold values from -0.5 to 0.5
Outputs:
- pair_result: float32 [256, 256, 128], P('row', 'col')
The draws below stay inside these ranges and needn't reach their ends.
All inputs are finite; a program needn't handle non-finite values.
Results may differ from the reference program's by a relative error of at most 0.0065.
Values may be sent and summed in bfloat16 or wider, within the bound.
No kernel may reach another device: no remote copies, remote signals or barrier semaphores. Data moves between devices by JAX's collectives and lax.ppermute only.
A program may use at most 128 MiB of HBM per device.

```python
import jax
import jax.numpy as jnp
from jax import lax

C = 128
CM = 64
CH = 32
CT = 128
S = 256
TOKENS_PER_ROW = 32
N = 256


def steps_of(rng, dims, pieces, low, high):
    gain, own = 1.0, jax.random.fold_in(rng, 6)
    for axis_at, shards_of in pieces:
        steps = jnp.exp(jax.random.uniform(jax.random.fold_in(own, axis_at), (shards_of,), jnp.float32, low / len(pieces), high / len(pieces)))
        gain = gain * jnp.repeat(steps, dims[axis_at] // shards_of).reshape([-1 if axis == axis_at else 1 for axis in range(len(dims))])
    return gain


def gaussian(rng, dims, scale, limit, cuts=(), kind=jnp.bfloat16):
    drawn = jax.random.normal(rng, dims, jnp.float32) * scale
    if len(cuts) > 0:
        drawn = steps_of(rng, dims, cuts, -0.22, 0.18) * drawn
    return jnp.clip(drawn, min=-limit, max=limit).astype(kind)


def setup_inputs(seed: int = 0) -> dict:
    key_list = jax.random.split(jax.random.key(seed), 9)
    return {
        "alignment": gaussian(key_list[0], (S, N * CM), 1.0, 6.0, ((0, 8), (1, 4))),
        "pair_state": gaussian(key_list[1], (N, N, C), 1.0, 6.0, ((0, 8), (1, 4)), jnp.float32),
        "alignment_factor_weight": gaussian(key_list[2], (CM, 2 * CH), CM ** -0.5, 0.75),
        "outer_proj": gaussian(key_list[3], (CH * CH, C), (max(1, CH * CH // S)) ** -0.5, 3.0),
        "outgoing_proj": gaussian(key_list[4], (C, 4 * CT + C), C ** -0.5, 0.5),
        "outgoing_final": gaussian(key_list[5], (CT, C), CT ** -0.5, 0.5),
        "incoming_proj": gaussian(key_list[6], (C, 4 * CT + C), C ** -0.5, 0.5),
        "incoming_final": gaussian(key_list[7], (CT, C), CT ** -0.5, 0.5),
    }


epsilon = 1e-05

def normalize_layer(values):
    average = lax.optimization_barrier(jnp.mean(values, axis=-1, keepdims=True))
    centred = values - average
    spread = lax.optimization_barrier(jnp.mean(centred * centred, axis=-1, keepdims=True))
    return centred * lax.rsqrt(spread + epsilon)

def triangle(pair_now, weights, final_weights, outgoing):
    hidden_dim = final_weights.shape[0]
    channels = pair_now.shape[-1]
    tokens = pair_now.shape[0]
    normed_in = normalize_layer(pair_now).astype(jnp.bfloat16).reshape(-1, channels)

    def project_cols(begin_col, end_col):
        result = jnp.dot(normed_in, weights[:, begin_col:end_col], preferred_element_type=jnp.float32)
        return result.reshape(tokens, tokens, end_col - begin_col)
    left_factor = (jax.nn.sigmoid(project_cols(0, hidden_dim)) * project_cols(hidden_dim, 2 * hidden_dim)).astype(jnp.bfloat16)
    right_factor = (jax.nn.sigmoid(project_cols(2 * hidden_dim, 3 * hidden_dim)) * project_cols(3 * hidden_dim, 4 * hidden_dim)).astype(jnp.bfloat16)
    gate_vals = jax.nn.sigmoid(project_cols(4 * hidden_dim, 4 * hidden_dim + channels))
    left_wide = left_factor.astype(jnp.float32)
    right_wide = right_factor.astype(jnp.float32)
    if outgoing:
        mixed_sum = jnp.einsum('ikc,jkc->ijc', left_wide, right_wide, precision=lax.Precision.HIGHEST)
    else:
        mixed_sum = jnp.einsum('kic,kjc->ijc', left_wide, right_wide, precision=lax.Precision.HIGHEST)
    normed_mix = normalize_layer(mixed_sum).astype(jnp.bfloat16).reshape(-1, hidden_dim)
    update = jnp.dot(normed_mix, final_weights, preferred_element_type=jnp.float32).reshape(tokens, tokens, channels)
    return pair_now + gate_vals * update

def reference(alignment, pair_state, alignment_factor_weight, outer_proj, outgoing_proj, outgoing_final, incoming_proj, incoming_final):
    tokens = pair_state.shape[0]
    seq_count = alignment.shape[0]
    feature_width = alignment_factor_weight.shape[0]
    hidden_outer = alignment_factor_weight.shape[1] // 2
    feature_values = alignment.astype(jnp.float32).reshape(seq_count, tokens, feature_width)
    normalized_alignment = normalize_layer(feature_values).astype(jnp.bfloat16).reshape(-1, feature_width)
    factor_pairs = jnp.dot(normalized_alignment, alignment_factor_weight, preferred_element_type=jnp.float32).astype(jnp.bfloat16)
    factor_pairs = factor_pairs.reshape(seq_count, tokens, 2 * hidden_outer)
    row_factor = factor_pairs[:, :, :hidden_outer].reshape(seq_count, tokens * hidden_outer)
    col_factor = factor_pairs[:, :, hidden_outer:].reshape(seq_count, tokens * hidden_outer)
    block_rows = TOKENS_PER_ROW
    block_count = tokens // block_rows

    def one_block(block_index):
        row_part = lax.dynamic_slice_in_dim(row_factor, block_index * (block_rows * hidden_outer), block_rows * hidden_outer, 1)
        outer_sum = jnp.dot(row_part.T, col_factor, preferred_element_type=jnp.float32) / seq_count
        outer_mean = outer_sum.astype(jnp.bfloat16).reshape(block_rows, hidden_outer, tokens, hidden_outer)
        outer_mean = outer_mean.transpose(0, 2, 1, 3).reshape(block_rows * tokens, hidden_outer * hidden_outer)
        return jnp.dot(outer_mean, outer_proj, preferred_element_type=jnp.float32).reshape(block_rows, tokens, -1)
    opm_term = lax.map(one_block, jnp.arange(block_count, dtype=jnp.int32)).reshape(tokens, tokens, -1)
    pair_opm = pair_state + opm_term
    pair_mid = triangle(pair_opm, outgoing_proj, outgoing_final, True)
    return triangle(pair_mid, incoming_proj, incoming_final, False)
```

```python
import functools

import jax
import jax.numpy as jnp
from jax import lax
from jax.experimental import pallas as pl
from jax.experimental.pallas import tpu as pltpu
from jax.sharding import PartitionSpec as P

EPS = 1e-05
LANES = 128
F32 = jnp.float32
BF16 = jnp.bfloat16


def contract(a, b, dim_a, dim_b):
    return lax.dot_general(a, b, (((dim_a,), (dim_b,)), ((), ())), preferred_element_type=F32)


def iota(shape, dim):
    return lax.broadcasted_iota(jnp.int32, shape, dim)


def call(kernel, out_shape, scratch, *args):
    return pl.pallas_call(
        kernel,
        out_shape=out_shape,
        in_specs=[pl.BlockSpec(memory_space=pltpu.VMEM)] * len(args),
        out_specs=jax.tree.map(lambda _: pl.BlockSpec(memory_space=pltpu.VMEM), out_shape),
        scratch_shapes=scratch,
    )(*args)


def factor_kernel(x_ref, w_ref, row_ref, col_ref):
    seq, width = x_ref.shape
    feats, both = w_ref.shape
    hid = both // 2
    per = LANES // hid
    span = per * feats
    groups = width // span
    blocks, _, row_width = row_ref.shape
    row_groups = row_width // LANES
    same = iota((span, span), 0) // feats == iota((span, span), 1) // feats
    spread = jnp.where(same, 1.0 / feats, 0.0).astype(BF16)
    x = jnp.concatenate([x_ref[:, g * span : (g + 1) * span] for g in range(groups)], axis=0)
    cen = x.astype(F32) - jnp.dot(x, spread, preferred_element_type=F32)
    sq = cen * cen
    high = sq.astype(BF16)
    low = (sq - high.astype(F32)).astype(BF16)
    var = jnp.dot(high, spread, preferred_element_type=F32) + jnp.dot(
        low, spread, preferred_element_type=F32
    )
    normed = (cen * lax.rsqrt(var + EPS)).astype(BF16)
    pick_rows = (iota((span, feats), 0) % feats == iota((span, feats), 1)).astype(BF16)
    col_id = iota((both, 2 * LANES), 1)
    pick_cols = (col_id // LANES * hid + col_id % hid == iota((both, 2 * LANES), 0)).astype(BF16)
    tall = jnp.dot(pick_rows, w_ref[...], preferred_element_type=F32).astype(BF16)
    wide = jnp.dot(tall, pick_cols, preferred_element_type=F32)
    mine = iota((span, 2 * LANES), 0) // feats == iota((span, 2 * LANES), 1) % LANES // hid
    weights = jnp.where(mine, wide, 0.0).astype(BF16)
    out = jnp.dot(normed, weights, preferred_element_type=F32).astype(BF16)
    for g in range(groups):
        piece = out[g * seq : (g + 1) * seq, :]
        at = g % row_groups * LANES
        row_ref[g // row_groups, :, at : at + LANES] = piece[:, :LANES]
        col_ref[:, g * LANES : (g + 1) * LANES] = piece[:, LANES:]


def widen_kernel(w_ref, out_ref, wide_ref, *, hid):
    per = LANES // hid
    channels = w_ref.shape[1]
    wide_ref[...] = w_ref[...].astype(F32)
    out_ref[...] = jnp.zeros_like(out_ref)
    for q in range(hid):
        part = wide_ref[pl.ds(q, hid, stride=hid), :].astype(BF16)
        for t in range(per):
            at = q * LANES + t * hid
            out_ref[at : at + hid, t * channels : (t + 1) * channels] = part


def normalize_rows(x):
    average = jnp.mean(x, axis=0, keepdims=True)
    cen = x - average
    return cen * lax.rsqrt(jnp.mean(cen * cen, axis=0, keepdims=True) + EPS)


def project(pair_ref, w_ref, lr_ref, gate_ref, left_ref, right_ref):
    channels, positions = pair_ref.shape
    groups = positions // LANES
    hid = (w_ref.shape[1] - channels) // 4
    count = lr_ref.shape[0]
    half = lr_ref.shape[1] // 2
    step = 4 * LANES
    for at in range(0, positions, step):
        normed = normalize_rows(pair_ref[:, at : at + step]).astype(BF16)

        def cols(begin, end):
            return contract(w_ref[:, begin:end], normed, 0, 0)

        left = jax.nn.sigmoid(cols(0, hid)) * cols(hid, 2 * hid)
        right = jax.nn.sigmoid(cols(2 * hid, 3 * hid)) * cols(3 * hid, 4 * hid)
        gate_ref[:, at : at + step] = jax.nn.sigmoid(cols(4 * hid, 4 * hid + channels))
        for g in range(at // LANES, (at + step) // LANES):
            lane = g * LANES - at
            left_ref[pl.ds(g, hid, stride=groups), :] = left[:, lane : lane + LANES]
            right_ref[pl.ds(g, hid, stride=groups), :] = right[:, lane : lane + LANES]
    lr_ref[:, :half, :] = left_ref[...].astype(BF16).reshape(count, half, LANES)
    lr_ref[:, half:, :] = right_ref[...].astype(BF16).reshape(count, half, LANES)


def opm_kernel(
    row_ref,
    col_ref,
    wide_ref,
    state_ref,
    w_ref,
    pair_ref,
    lr_ref,
    gate_ref,
    row_scr,
    outer_scr,
    lhs_scr,
    left_scr,
    right_scr,
    *,
    hid,
):
    blocks, seq, row_width = row_ref.shape
    row_tokens, col_tokens, channels = state_ref.shape
    total = blocks * seq
    per = LANES // hid
    mine = lax.axis_index("row")
    for m in range(blocks):
        row_scr[m * seq : (m + 1) * seq, :] = row_ref[mine ^ m]
    pack = LANES // col_tokens
    groups = row_tokens // per
    pairs = groups // pack
    tall = col_tokens * hid
    outer = contract(col_ref[...].reshape(total, tall), row_scr[...], 0, 0)
    for g in range(groups):
        outer_scr[g * tall : (g + 1) * tall, :] = outer[:, g * LANES : (g + 1) * LANES]
    for q in range(hid):
        for g in range(groups):
            part = outer_scr[pl.ds(g * tall + q, col_tokens, stride=hid), :] * (1.0 / total)
            at = (g % pairs * pack + g // pairs) * col_tokens
            lhs_scr[at : at + col_tokens, q * LANES : (q + 1) * LANES] = part.astype(BF16)
    term = jnp.dot(lhs_scr[...], wide_ref[...], preferred_element_type=F32)
    half = row_tokens // pack
    for g in range(pairs):
        for t in range(per):
            token = g * per + t
            block = term[g * LANES : (g + 1) * LANES, t * channels : (t + 1) * channels]
            state = jnp.concatenate([state_ref[token + h * half] for h in range(pack)], axis=0)
            pair_ref[:, token * LANES : (token + 1) * LANES] = (block + state).T
    project(pair_ref, w_ref, lr_ref, gate_ref, left_scr, right_scr)


def mix_kernel(lr_ref, out_ref, left_scr, right_scr, *, rows, cols, row_tokens, col_tokens, outgoing):
    pack = LANES // col_tokens
    half = row_tokens // pack
    share = out_ref.shape[1] // half
    for e in range(share):
        for part, scr in enumerate((left_scr, right_scr)):
            at = (part * share + e) * half
            for r in range(rows):
                for m in range(cols // pack):
                    tiles = [
                        lr_ref[r * cols + m * pack + b, at : at + half, :] for b in range(pack)
                    ]
                    for h in range(pack):
                        joined = jnp.concatenate(
                            [tile[:, h * col_tokens : (h + 1) * col_tokens] for tile in tiles], axis=1
                        )
                        first = r * row_tokens + h * half
                        scr[first : first + half, m * LANES : (m + 1) * LANES] = joined
        dim = 1 if outgoing else 0
        mixed = contract(left_scr[...], right_scr[...], dim, dim).astype(BF16)
        for r in range(rows):
            for m in range(cols // pack):
                tiles = [
                    mixed[
                        r * row_tokens + h * half : r * row_tokens + (h + 1) * half,
                        m * LANES : (m + 1) * LANES,
                    ]
                    for h in range(pack)
                ]
                for b in range(pack):
                    joined = jnp.concatenate(
                        [tile[:, b * col_tokens : (b + 1) * col_tokens] for tile in tiles], axis=1
                    )
                    out_ref[r * cols + m * pack + b, e * half : (e + 1) * half, :] = joined


def normalize_mix(mix_ref, scr, hid, groups):
    mixed = mix_ref[...].reshape(hid, groups, LANES).astype(F32)
    average = jnp.mean(mixed, axis=0, keepdims=True)
    cen = mixed - average
    spread = jnp.mean(cen * cen, axis=0, keepdims=True)
    scr[...] = (cen * lax.rsqrt(spread + EPS)).reshape(hid * groups, LANES)


def update_group(scr, final_ref, g, groups):
    hid = final_ref.shape[0]
    normed = scr[pl.ds(g, hid, stride=groups), :].astype(BF16)
    return contract(final_ref[...], normed, 0, 0)


def finish_kernel(
    mix_ref, pair_ref, gate_ref, final_ref, w_ref, mid_ref, lr_ref, gate_out_ref, scr, left_scr, right_scr
):
    hid = final_ref.shape[0]
    groups = pair_ref.shape[1] // LANES
    normalize_mix(mix_ref, scr, hid, groups)
    for g in range(groups):
        at = slice(g * LANES, (g + 1) * LANES)
        mid_ref[:, at] = pair_ref[:, at] + gate_ref[:, at] * update_group(scr, final_ref, g, groups)
    project(mid_ref, w_ref, lr_ref, gate_out_ref, left_scr, right_scr)


def last_kernel(mix_ref, pair_ref, gate_ref, final_ref, out_ref, scr):
    hid = final_ref.shape[0]
    row_tokens, col_tokens, _ = out_ref.shape
    groups = pair_ref.shape[1] // LANES
    pack = LANES // col_tokens
    normalize_mix(mix_ref, scr, hid, groups)
    for g in range(groups):
        at = slice(g * LANES, (g + 1) * LANES)
        done = pair_ref[:, at] + gate_ref[:, at] * update_group(scr, final_ref, g, groups)
        done = done.T
        for h in range(pack):
            out_ref[g + h * groups] = done[h * col_tokens : (h + 1) * col_tokens, :]


def gather_blocks(block, rows):
    far = [block] + [
        lax.ppermute(block, "row", [(i, i ^ m) for i in range(rows)]) for m in range(2, rows, 2)
    ]
    far = jnp.stack(far)
    near = lax.ppermute(far, "row", [(i, i ^ 1) for i in range(rows)])
    return jnp.stack([far, near], axis=1).reshape((rows,) + block.shape)


def local(
    alignment,
    pair_state,
    alignment_factor_weight,
    outer_proj,
    outgoing_proj,
    outgoing_final,
    incoming_proj,
    incoming_final,
):
    seq = alignment.shape[0]
    row_tokens, col_tokens, channels = pair_state.shape
    hid_outer = alignment_factor_weight.shape[1] // 2
    hid = outgoing_final.shape[0]
    rows, cols = lax.axis_size("row"), lax.axis_size("col")
    count = rows * cols
    total = rows * seq
    per = LANES // hid_outer
    positions = row_tokens * col_tokens
    groups = positions // LANES
    both = ("row", "col")
    shape = jax.ShapeDtypeStruct

    row_source, col_source = call(
        factor_kernel,
        (
            shape((col_tokens // row_tokens, seq, row_tokens * hid_outer), BF16),
            shape((seq, col_tokens * hid_outer), BF16),
        ),
        [],
        alignment,
        alignment_factor_weight,
    )
    wide = call(
        functools.partial(widen_kernel, hid=hid_outer),
        shape((hid_outer * LANES, per * channels), BF16),
        [pltpu.VMEM(outer_proj.shape, F32)],
        outer_proj,
    )
    col_all = gather_blocks(col_source, rows)
    row_all = lax.all_gather(row_source, "col", axis=0, tiled=True)
    row_all = lax.all_to_all(row_all, "row", split_axis=0, concat_axis=0, tiled=True)

    state = shape((channels, positions), F32)
    wire = shape((count, 2 * hid // count * groups, LANES), BF16)
    turned = pltpu.VMEM((hid * groups, LANES), F32)
    pair, factors, gate = call(
        functools.partial(opm_kernel, hid=hid_outer),
        (state, wire, state),
        [
            pltpu.VMEM((total, row_tokens * hid_outer), BF16),
            pltpu.VMEM((positions * hid_outer * hid_outer // LANES, LANES), F32),
            pltpu.VMEM((positions // per, hid_outer * LANES), BF16),
            turned,
            turned,
        ],
        row_all,
        col_all,
        wide,
        pair_state,
        outgoing_proj,
    )

    def mix(factors, outgoing):
        factors = lax.all_to_all(factors, both, split_axis=0, concat_axis=0, tiled=True)
        whole = (rows * row_tokens, cols * col_tokens)
        mixed = call(
            functools.partial(
                mix_kernel,
                rows=rows,
                cols=cols,
                row_tokens=row_tokens,
                col_tokens=col_tokens,
                outgoing=outgoing,
            ),
            shape((count, hid // count * groups, LANES), BF16),
            [pltpu.VMEM(whole, BF16)] * 2,
            factors,
        )
        return lax.all_to_all(mixed, both, split_axis=0, concat_axis=0, tiled=True)

    pair, factors, gate = call(
        finish_kernel,
        (state, wire, state),
        [turned, turned, turned],
        mix(factors, True),
        pair,
        gate,
        outgoing_final,
        incoming_proj,
    )
    return call(
        last_kernel,
        shape(pair_state.shape, F32),
        [turned],
        mix(factors, False),
        pair,
        gate,
        incoming_final,
    )


def solution(mesh):
    return jax.shard_map(
        local,
        mesh=mesh,
        in_specs=(P("row", "col"), P("row", "col", None), P(), P(), P(), P(), P(), P()),
        out_specs=P("row", "col", None),
        check_vma=False,
    )
```

```python
import functools

import jax
import jax.numpy as jnp
from jax import lax
from jax.experimental import pallas as pl
from jax.experimental.pallas import tpu as pltpu
from jax.sharding import PartitionSpec as P

EPS = 1e-05
LANES = 128
SCOPED = 28 << 20
F32 = jnp.float32
BF16 = jnp.bfloat16


def contract(a, b, dim_a, dim_b):
    return lax.dot_general(a, b, (((dim_a,), (dim_b,)), ((), ())), preferred_element_type=F32)


def iota(shape, dim):
    return lax.broadcasted_iota(jnp.int32, shape, dim)


def call(kernel, out_shape, scratch, *args, keep=True):
    space = pltpu.VMEM if keep else pltpu.HBM
    return pl.pallas_call(
        kernel,
        out_shape=jax.tree.map(lambda o: space(o.shape, o.dtype), out_shape),
        in_specs=[pl.BlockSpec(memory_space=pltpu.VMEM)] * len(args),
        out_specs=jax.tree.map(lambda _: pl.BlockSpec(memory_space=pltpu.VMEM), out_shape),
        scratch_shapes=scratch,
        compiler_params=pltpu.CompilerParams(vmem_limit_bytes=SCOPED),
    )(*args)


def near(array):
    return pltpu.with_memory_space_constraint(array, pltpu.VMEM)


def factor_kernel(x_ref, w_ref, col_ref, *rest, cols, blocks):
    pieces, row_scr = rest[:-1], rest[-1]
    seq, width = x_ref.shape
    feats, both = w_ref.shape
    hid = both // 2
    per = LANES // hid
    span = per * feats
    groups = width // span
    row_groups = groups // blocks
    slice_rows = seq // cols
    same = iota((span, span), 0) // feats == iota((span, span), 1) // feats
    spread = jnp.where(same, 1.0 / feats, 0.0).astype(BF16)
    x = jnp.concatenate([x_ref[:, g * span : (g + 1) * span] for g in range(groups)], axis=0)
    cen = x.astype(F32) - jnp.dot(x, spread, preferred_element_type=F32)
    sq = cen * cen
    high = sq.astype(BF16)
    low = (sq - high.astype(F32)).astype(BF16)
    var = jnp.dot(high, spread, preferred_element_type=F32) + jnp.dot(
        low, spread, preferred_element_type=F32
    )
    normed = (cen * lax.rsqrt(var + EPS)).astype(BF16)
    pick_rows = (iota((span, feats), 0) % feats == iota((span, feats), 1)).astype(BF16)
    col_id = iota((both, 2 * LANES), 1)
    pick_cols = (col_id // LANES * hid + col_id % hid == iota((both, 2 * LANES), 0)).astype(BF16)
    tall = jnp.dot(pick_rows, w_ref[...], preferred_element_type=F32).astype(BF16)
    wide = jnp.dot(tall, pick_cols, preferred_element_type=F32)
    mine = iota((span, 2 * LANES), 0) // feats == iota((span, 2 * LANES), 1) % LANES // hid
    weights = jnp.where(mine, wide, 0.0).astype(BF16)
    out = jnp.dot(normed, weights, preferred_element_type=F32).astype(BF16)
    for g in range(groups):
        piece = out[g * seq : (g + 1) * seq, :]
        at = g % row_groups * LANES
        block = g // row_groups
        for c in range(cols):
            row_scr[block * cols + c, :, at : at + LANES] = piece[
                c * slice_rows : (c + 1) * slice_rows, :LANES
            ].astype(F32)
        col_ref[:, g * LANES : (g + 1) * LANES] = piece[:, LANES:]
    mine = lax.axis_index("row")
    for n, ref in enumerate(pieces):
        block = (mine // cols + n // cols) % blocks
        c = (mine % cols + n % cols) % cols
        ref[...] = row_scr[block * cols + c].astype(BF16)


def widen_kernel(w_ref, out_ref, wide_ref, *, hid, scale):
    per = LANES // hid // 2
    channels = w_ref.shape[1]
    wide_ref[...] = w_ref[...].astype(F32) * scale
    out_ref[...] = jnp.zeros_like(out_ref)
    for q in range(hid):
        part = wide_ref[pl.ds(q, hid, stride=hid), :].astype(BF16)
        for t in range(per):
            at = q % (hid // 2) * LANES + (q // (hid // 2) * per + t) * hid
            out_ref[at : at + hid, t * channels : (t + 1) * channels] = part


def normalize_rows(x):
    average = jnp.mean(x, axis=0, keepdims=True)
    cen = x - average
    return cen * lax.rsqrt(jnp.mean(cen * cen, axis=0, keepdims=True) + EPS)


def project(pair_ref, w_ref, lr_ref, gate_ref, left_ref, right_ref):
    channels, positions = pair_ref.shape
    groups = positions // LANES
    hid = (w_ref.shape[1] - channels) // 4
    count = lr_ref.shape[0]
    half = lr_ref.shape[1] // 2
    step = 2 * LANES
    for at in range(0, positions, step):
        normed = normalize_rows(pair_ref[:, at : at + step]).astype(BF16)

        def cols(begin, end):
            return contract(w_ref[:, begin:end], normed, 0, 0)

        left = jax.nn.sigmoid(cols(0, hid)) * cols(hid, 2 * hid)
        right = jax.nn.sigmoid(cols(2 * hid, 3 * hid)) * cols(3 * hid, 4 * hid)
        gate_ref[:, at : at + step] = jax.nn.sigmoid(cols(4 * hid, 4 * hid + channels))
        for g in range(at // LANES, (at + step) // LANES):
            lane = g * LANES - at
            left_ref[pl.ds(g, hid, stride=groups), :] = left[:, lane : lane + LANES]
            right_ref[pl.ds(g, hid, stride=groups), :] = right[:, lane : lane + LANES]
    lr_ref[:, :half, :] = left_ref[...].astype(BF16).reshape(count, half, LANES)
    lr_ref[:, half:, :] = right_ref[...].astype(BF16).reshape(count, half, LANES)


def opm_kernel(row_ref, wide_ref, state_ref, w_ref, *rest, hid, rows, cols):
    col_refs = rest[:rows]
    pair_ref, lr_ref, gate_ref, row_scr, col_scr, outer_scr, lhs_scr, left_scr, right_scr = rest[rows:]
    _, slice_rows, row_width = row_ref.shape
    row_tokens, col_tokens, channels = state_ref.shape
    seq = slice_rows * cols
    blocks = rows // cols
    tall = col_tokens * hid
    row_at = lax.axis_index("row")
    for m in range(rows):
        source = row_at ^ m
        block = (row_at % blocks + blocks - source // cols) % blocks
        for c in range(cols):
            turn = (c + cols - source % cols) % cols
            piece = row_ref[c * rows + block * cols + turn]
            at = m * seq + c * slice_rows
            row_scr[at : at + slice_rows, :] = piece
        col_scr[:, m * seq : (m + 1) * seq] = col_refs[m][...].T
    groups = row_tokens * hid // LANES
    for n in range(groups // 2):
        part = row_scr[:, n * 2 * LANES : (n + 1) * 2 * LANES]
        for at in range(0, tall, 512):
            outer = jnp.dot(col_scr[at : at + 512, :], part, preferred_element_type=F32)
            for b in range(2):
                first = (2 * n + b) * tall + at
                outer_scr[first : first + 512, :] = outer[:, b * LANES : (b + 1) * LANES]
    per = LANES // hid // 2
    pack = LANES // col_tokens
    fold = row_tokens // per // pack
    half_lanes = LANES // 2
    for q in range(hid // 2):
        for g in range(groups):
            first = outer_scr[pl.ds(g * tall + q, col_tokens, stride=hid), :].astype(BF16)
            second = outer_scr[pl.ds(g * tall + q + hid // 2, col_tokens, stride=hid), :].astype(BF16)
            for b in range(2):
                lanes = slice(b * half_lanes, (b + 1) * half_lanes)
                joined = jnp.concatenate([first[:, lanes], second[:, lanes]], axis=1)
                unit = 2 * g + b
                at = (unit % fold * pack + unit // fold) * col_tokens
                lhs_scr[at : at + col_tokens, q * LANES : (q + 1) * LANES] = joined
    term = jnp.dot(lhs_scr[...], wide_ref[...], preferred_element_type=F32)
    half = row_tokens // pack
    for g in range(fold):
        for t in range(per):
            token = g * per + t
            block = term[g * LANES : (g + 1) * LANES, t * channels : (t + 1) * channels]
            state = jnp.concatenate([state_ref[token + h * half] for h in range(pack)], axis=0)
            pair_ref[:, token * LANES : (token + 1) * LANES] = (block + state).T
    project(pair_ref, w_ref, lr_ref, gate_ref, left_scr, right_scr)


def mix_kernel(lr_ref, out_ref, left_scr, right_scr, *, rows, cols, row_tokens, col_tokens, outgoing):
    pack = LANES // col_tokens
    half = row_tokens // pack
    share = out_ref.shape[1] // half
    for e in range(share):
        for part, scr in enumerate((left_scr, right_scr)):
            at = (part * share + e) * half
            for r in range(rows):
                for m in range(cols // pack):
                    tiles = [
                        lr_ref[r * cols + m * pack + b, at : at + half, :] for b in range(pack)
                    ]
                    for h in range(pack):
                        joined = jnp.concatenate(
                            [tile[:, h * col_tokens : (h + 1) * col_tokens] for tile in tiles], axis=1
                        )
                        first = r * row_tokens + h * half
                        scr[first : first + half, m * LANES : (m + 1) * LANES] = joined
        dim = 1 if outgoing else 0
        mixed = contract(left_scr[...], right_scr[...], dim, dim).astype(BF16)
        for r in range(rows):
            for m in range(cols // pack):
                tiles = [
                    mixed[
                        r * row_tokens + h * half : r * row_tokens + (h + 1) * half,
                        m * LANES : (m + 1) * LANES,
                    ]
                    for h in range(pack)
                ]
                for b in range(pack):
                    joined = jnp.concatenate(
                        [tile[:, b * col_tokens : (b + 1) * col_tokens] for tile in tiles], axis=1
                    )
                    out_ref[r * cols + m * pack + b, e * half : (e + 1) * half, :] = joined


def normalize_mix(mix_ref, scr, hid, groups):
    mixed = mix_ref[...].reshape(hid, groups, LANES).astype(F32)
    average = jnp.mean(mixed, axis=0, keepdims=True)
    cen = mixed - average
    spread = jnp.mean(cen * cen, axis=0, keepdims=True)
    scr[...] = (cen * lax.rsqrt(spread + EPS)).reshape(hid * groups, LANES)


def update_group(scr, final_ref, g, groups):
    hid = final_ref.shape[0]
    normed = scr[pl.ds(g, hid, stride=groups), :].astype(BF16)
    return contract(final_ref[...], normed, 0, 0)


def finish_kernel(
    mix_ref, pair_ref, gate_ref, final_ref, w_ref, mid_ref, lr_ref, gate_out_ref, scr, left_scr, right_scr
):
    hid = final_ref.shape[0]
    groups = pair_ref.shape[1] // LANES
    normalize_mix(mix_ref, scr, hid, groups)
    for g in range(groups):
        at = slice(g * LANES, (g + 1) * LANES)
        mid_ref[:, at] = pair_ref[:, at] + gate_ref[:, at] * update_group(scr, final_ref, g, groups)
    project(mid_ref, w_ref, lr_ref, gate_out_ref, left_scr, right_scr)


def last_kernel(mix_ref, pair_ref, gate_ref, final_ref, out_ref, scr):
    hid = final_ref.shape[0]
    row_tokens, col_tokens, _ = out_ref.shape
    groups = pair_ref.shape[1] // LANES
    pack = LANES // col_tokens
    normalize_mix(mix_ref, scr, hid, groups)
    for g in range(groups):
        at = slice(g * LANES, (g + 1) * LANES)
        done = pair_ref[:, at] + gate_ref[:, at] * update_group(scr, final_ref, g, groups)
        done = done.T
        for h in range(pack):
            out_ref[g + h * groups] = done[h * col_tokens : (h + 1) * col_tokens, :]


def gather_blocks(block, rows):
    found = []
    for m in range(0, rows, 2):
        far = block
        if m > 0:
            far = lax.ppermute(block, "row", [(i, i ^ m) for i in range(rows)])
        found += [far, lax.ppermute(far, "row", [(i, i ^ 1) for i in range(rows)])]
    return found


def gather_rows(pieces, rows, cols):
    blocks = rows // cols
    landed = []
    for n, piece in enumerate(pieces):
        pairs = []
        for r in range(rows):
            for c in range(cols):
                to_row = c * blocks + (r // cols + n // cols) % blocks
                pairs.append((r * cols + c, to_row * cols + (r % cols + n % cols) % cols))
        landed.append(lax.ppermute(piece, ("row", "col"), pairs))
    return lax.all_gather(jnp.stack(landed), "col", axis=0, tiled=True)


def local(
    alignment,
    pair_state,
    alignment_factor_weight,
    outer_proj,
    outgoing_proj,
    outgoing_final,
    incoming_proj,
    incoming_final,
):
    seq = alignment.shape[0]
    row_tokens, col_tokens, channels = pair_state.shape
    hid_outer = alignment_factor_weight.shape[1] // 2
    hid = outgoing_final.shape[0]
    rows, cols = lax.axis_size("row"), lax.axis_size("col")
    count = rows * cols
    total = rows * seq
    per = LANES // hid_outer
    positions = row_tokens * col_tokens
    groups = positions // LANES
    both = ("row", "col")
    shape = jax.ShapeDtypeStruct

    blocks = rows // cols
    piece = shape((seq // cols, row_tokens * hid_outer), BF16)
    col_source, *pieces = call(
        functools.partial(factor_kernel, cols=cols, blocks=blocks),
        (shape((seq, col_tokens * hid_outer), BF16),) + (piece,) * rows,
        [pltpu.VMEM((rows,) + piece.shape, F32)],
        alignment,
        alignment_factor_weight,
    )
    wide = call(
        functools.partial(widen_kernel, hid=hid_outer, scale=1.0 / total),
        shape((hid_outer // 2 * LANES, per // 2 * channels), BF16),
        [pltpu.VMEM(outer_proj.shape, F32)],
        outer_proj,
    )
    col_all = gather_blocks(col_source, rows)
    row_all = gather_rows(pieces, rows, cols)

    state = shape((channels, positions), F32)
    wire = shape((count, 2 * hid // count * groups, LANES), BF16)
    turned = pltpu.VMEM((hid * groups, LANES), F32)
    pair, factors, gate = call(
        functools.partial(opm_kernel, hid=hid_outer, rows=rows, cols=cols),
        (state, wire, state),
        [
            pltpu.VMEM((total, row_tokens * hid_outer), BF16),
            pltpu.VMEM((col_tokens * hid_outer, total), BF16),
            pltpu.VMEM((positions * hid_outer * hid_outer // LANES, LANES), F32),
            pltpu.VMEM((positions * 2 // per, hid_outer // 2 * LANES), BF16),
            turned,
            turned,
        ],
        row_all,
        wide,
        near(pair_state),
        near(outgoing_proj),
        *col_all,
    )

    def mix(factors, outgoing):
        factors = lax.all_to_all(factors, both, split_axis=0, concat_axis=0, tiled=True)
        whole = (rows * row_tokens, cols * col_tokens)
        mixed = call(
            functools.partial(
                mix_kernel,
                rows=rows,
                cols=cols,
                row_tokens=row_tokens,
                col_tokens=col_tokens,
                outgoing=outgoing,
            ),
            shape((count, hid // count * groups, LANES), BF16),
            [pltpu.VMEM(whole, BF16)] * 2,
            factors,
        )
        return lax.all_to_all(mixed, both, split_axis=0, concat_axis=0, tiled=True)

    pair, factors, gate = call(
        finish_kernel,
        (state, wire, state),
        [turned, turned, turned],
        mix(factors, True),
        pair,
        gate,
        near(outgoing_final),
        near(incoming_proj),
    )
    return call(
        last_kernel,
        shape(pair_state.shape, F32),
        [turned],
        mix(factors, False),
        pair,
        gate,
        near(incoming_final),
        keep=False,
    )


def solution(mesh):
    return jax.shard_map(
        local,
        mesh=mesh,
        in_specs=(P("row", "col"), P("row", "col", None), P(), P(), P(), P(), P(), P()),
        out_specs=P("row", "col", None),
        check_vma=False,
    )
```

```python
import functools

import jax
import jax.numpy as jnp
from jax import lax
from jax.experimental import pallas as pl
from jax.experimental.pallas import tpu as pltpu
from jax.sharding import PartitionSpec as P

EPS = 1e-05
LANES = 128
SCOPED = 28 << 20
F32 = jnp.float32
BF16 = jnp.bfloat16


def contract(a, b, dim_a, dim_b):
    return lax.dot_general(a, b, (((dim_a,), (dim_b,)), ((), ())), preferred_element_type=F32)


def iota(shape, dim):
    return lax.broadcasted_iota(jnp.int32, shape, dim)


def call(kernel, out_shape, scratch, *args, keep=True):
    space = pltpu.VMEM if keep else pltpu.HBM
    return pl.pallas_call(
        kernel,
        out_shape=jax.tree.map(lambda o: space(o.shape, o.dtype), out_shape),
        in_specs=[pl.BlockSpec(memory_space=pltpu.VMEM)] * len(args),
        out_specs=jax.tree.map(lambda _: pl.BlockSpec(memory_space=pltpu.VMEM), out_shape),
        scratch_shapes=scratch,
        compiler_params=pltpu.CompilerParams(vmem_limit_bytes=SCOPED),
    )(*args)


def near(array):
    return pltpu.with_memory_space_constraint(array, pltpu.VMEM)


def factor_kernel(x_ref, w_ref, row_ref, col_ref):
    cols, blocks = row_ref.shape[:2]
    seq, width = x_ref.shape
    feats, both = w_ref.shape
    hid = both // 2
    per = LANES // hid
    span = per * feats
    groups = width // span
    row_groups = groups // blocks
    slice_rows = seq // cols
    same = iota((span, span), 0) // feats == iota((span, span), 1) // feats
    spread = jnp.where(same, 1.0 / feats, 0.0).astype(BF16)
    x = jnp.concatenate([x_ref[:, g * span : (g + 1) * span] for g in range(groups)], axis=0)
    cen = x.astype(F32) - jnp.dot(x, spread, preferred_element_type=F32)
    sq = cen * cen
    high = sq.astype(BF16)
    low = (sq - high.astype(F32)).astype(BF16)
    var = jnp.dot(high, spread, preferred_element_type=F32) + jnp.dot(
        low, spread, preferred_element_type=F32
    )
    normed = (cen * lax.rsqrt(var + EPS)).astype(BF16)
    pick_rows = (iota((span, feats), 0) % feats == iota((span, feats), 1)).astype(BF16)
    col_id = iota((both, 2 * LANES), 1)
    pick_cols = (col_id // LANES * hid + col_id % hid == iota((both, 2 * LANES), 0)).astype(BF16)
    tall = jnp.dot(pick_rows, w_ref[...], preferred_element_type=F32).astype(BF16)
    wide = jnp.dot(tall, pick_cols, preferred_element_type=F32)
    mine = iota((span, 2 * LANES), 0) // feats == iota((span, 2 * LANES), 1) % LANES // hid
    weights = jnp.where(mine, wide, 0.0).astype(BF16)
    out = jnp.dot(normed, weights, preferred_element_type=F32).astype(BF16)
    for g in range(groups):
        piece = out[g * seq : (g + 1) * seq, :]
        at = g % row_groups * LANES
        block = g // row_groups
        for c in range(cols):
            row_ref[c, block, :, at : at + LANES] = piece[
                c * slice_rows : (c + 1) * slice_rows, :LANES
            ]
        col_ref[:, g * LANES : (g + 1) * LANES] = piece[:, LANES:]


def widen_kernel(w_ref, out_ref, wide_ref, *, hid, scale):
    per = LANES // hid // 2
    channels = w_ref.shape[1]
    wide_ref[...] = w_ref[...].astype(F32) * scale
    out_ref[...] = jnp.zeros_like(out_ref)
    for q in range(hid):
        part = wide_ref[pl.ds(q, hid, stride=hid), :].astype(BF16)
        for t in range(per):
            at = q % (hid // 2) * LANES + (q // (hid // 2) * per + t) * hid
            out_ref[at : at + hid, t * channels : (t + 1) * channels] = part


def normalize_rows(x):
    average = jnp.mean(x, axis=0, keepdims=True)
    cen = x - average
    return cen * lax.rsqrt(jnp.mean(cen * cen, axis=0, keepdims=True) + EPS)


def project(pair_ref, w_ref, lr_ref, gate_ref, left_ref, right_ref):
    channels, positions = pair_ref.shape
    groups = positions // LANES
    hid = (w_ref.shape[1] - channels) // 4
    count = lr_ref.shape[0]
    half = lr_ref.shape[1] // 2
    step = 2 * LANES
    for at in range(0, positions, step):
        normed = normalize_rows(pair_ref[:, at : at + step]).astype(BF16)

        def cols(begin, end):
            return contract(w_ref[:, begin:end], normed, 0, 0)

        left = jax.nn.sigmoid(cols(0, hid)) * cols(hid, 2 * hid)
        right = jax.nn.sigmoid(cols(2 * hid, 3 * hid)) * cols(3 * hid, 4 * hid)
        gate_ref[:, at : at + step] = jax.nn.sigmoid(cols(4 * hid, 4 * hid + channels))
        for g in range(at // LANES, (at + step) // LANES):
            lane = g * LANES - at
            left_ref[pl.ds(g, hid, stride=groups), :] = left[:, lane : lane + LANES]
            right_ref[pl.ds(g, hid, stride=groups), :] = right[:, lane : lane + LANES]
    lr_ref[:, :half, :] = left_ref[...].astype(BF16).reshape(count, half, LANES)
    lr_ref[:, half:, :] = right_ref[...].astype(BF16).reshape(count, half, LANES)


def opm_kernel(row_ref, wide_ref, state_ref, w_ref, *rest, hid, rows, cols):
    col_refs = rest[:rows]
    pair_ref, lr_ref, gate_ref, row_scr, col_scr, outer_scr, lhs_scr, left_scr, right_scr = rest[rows:]
    _, slice_rows, row_width = row_ref.shape
    row_tokens, col_tokens, channels = state_ref.shape
    seq = slice_rows * cols
    tall = col_tokens * hid
    row_at = lax.axis_index("row")
    for m in range(rows):
        source = row_at ^ m
        for c in range(cols):
            at = m * seq + c * slice_rows
            row_scr[at : at + slice_rows, :] = row_ref[c * rows + source]
        col_scr[:, m * seq : (m + 1) * seq] = col_refs[m][...].T
    groups = row_tokens * hid // LANES
    for n in range(groups // 2):
        part = row_scr[:, n * 2 * LANES : (n + 1) * 2 * LANES]
        for at in range(0, tall, 512):
            outer = jnp.dot(col_scr[at : at + 512, :], part, preferred_element_type=F32)
            for b in range(2):
                first = (2 * n + b) * tall + at
                outer_scr[first : first + 512, :] = outer[:, b * LANES : (b + 1) * LANES]
    per = LANES // hid // 2
    pack = LANES // col_tokens
    fold = row_tokens // per // pack
    half_lanes = LANES // 2
    for q in range(hid // 2):
        for g in range(groups):
            first = outer_scr[pl.ds(g * tall + q, col_tokens, stride=hid), :].astype(BF16)
            second = outer_scr[pl.ds(g * tall + q + hid // 2, col_tokens, stride=hid), :].astype(BF16)
            for b in range(2):
                lanes = slice(b * half_lanes, (b + 1) * half_lanes)
                joined = jnp.concatenate([first[:, lanes], second[:, lanes]], axis=1)
                unit = 2 * g + b
                at = (unit % fold * pack + unit // fold) * col_tokens
                lhs_scr[at : at + col_tokens, q * LANES : (q + 1) * LANES] = joined
    term = jnp.dot(lhs_scr[...], wide_ref[...], preferred_element_type=F32)
    half = row_tokens // pack
    for g in range(fold):
        for t in range(per):
            token = g * per + t
            block = term[g * LANES : (g + 1) * LANES, t * channels : (t + 1) * channels]
            state = jnp.concatenate([state_ref[token + h * half] for h in range(pack)], axis=0)
            pair_ref[:, token * LANES : (token + 1) * LANES] = (block + state).T
    project(pair_ref, w_ref, lr_ref, gate_ref, left_scr, right_scr)


def mix_kernel(lr_ref, out_ref, left_scr, right_scr, *, rows, cols, row_tokens, col_tokens, outgoing):
    pack = LANES // col_tokens
    half = row_tokens // pack
    share = out_ref.shape[1] // half
    for e in range(share):
        for part, scr in enumerate((left_scr, right_scr)):
            at = (part * share + e) * half
            for r in range(rows):
                for m in range(cols // pack):
                    tiles = [
                        lr_ref[r * cols + m * pack + b, at : at + half, :] for b in range(pack)
                    ]
                    for h in range(pack):
                        joined = jnp.concatenate(
                            [tile[:, h * col_tokens : (h + 1) * col_tokens] for tile in tiles], axis=1
                        )
                        first = r * row_tokens + h * half
                        scr[first : first + half, m * LANES : (m + 1) * LANES] = joined
        dim = 1 if outgoing else 0
        mixed = contract(left_scr[...], right_scr[...], dim, dim).astype(BF16)
        for r in range(rows):
            for m in range(cols // pack):
                tiles = [
                    mixed[
                        r * row_tokens + h * half : r * row_tokens + (h + 1) * half,
                        m * LANES : (m + 1) * LANES,
                    ]
                    for h in range(pack)
                ]
                for b in range(pack):
                    joined = jnp.concatenate(
                        [tile[:, b * col_tokens : (b + 1) * col_tokens] for tile in tiles], axis=1
                    )
                    out_ref[r * cols + m * pack + b, e * half : (e + 1) * half, :] = joined


def normalize_mix(mix_ref, scr, hid, groups):
    mixed = mix_ref[...].reshape(hid, groups, LANES).astype(F32)
    average = jnp.mean(mixed, axis=0, keepdims=True)
    cen = mixed - average
    spread = jnp.mean(cen * cen, axis=0, keepdims=True)
    scr[...] = (cen * lax.rsqrt(spread + EPS)).reshape(hid * groups, LANES)


def update_group(scr, final_ref, g, groups):
    hid = final_ref.shape[0]
    normed = scr[pl.ds(g, hid, stride=groups), :].astype(BF16)
    return contract(final_ref[...], normed, 0, 0)


def finish_kernel(
    mix_ref, pair_ref, gate_ref, final_ref, w_ref, mid_ref, lr_ref, gate_out_ref, scr, left_scr, right_scr
):
    hid = final_ref.shape[0]
    groups = pair_ref.shape[1] // LANES
    normalize_mix(mix_ref, scr, hid, groups)
    for g in range(groups):
        at = slice(g * LANES, (g + 1) * LANES)
        mid_ref[:, at] = pair_ref[:, at] + gate_ref[:, at] * update_group(scr, final_ref, g, groups)
    project(mid_ref, w_ref, lr_ref, gate_out_ref, left_scr, right_scr)


def last_kernel(mix_ref, pair_ref, gate_ref, final_ref, out_ref, scr):
    hid = final_ref.shape[0]
    row_tokens, col_tokens, _ = out_ref.shape
    groups = pair_ref.shape[1] // LANES
    pack = LANES // col_tokens
    normalize_mix(mix_ref, scr, hid, groups)
    for g in range(groups):
        at = slice(g * LANES, (g + 1) * LANES)
        done = pair_ref[:, at] + gate_ref[:, at] * update_group(scr, final_ref, g, groups)
        done = done.T
        for h in range(pack):
            out_ref[g + h * groups] = done[h * col_tokens : (h + 1) * col_tokens, :]


def gather_blocks(block, rows):
    found = []
    for m in range(0, rows, 2):
        far = block
        if m > 0:
            far = lax.ppermute(block, "row", [(i, i ^ m) for i in range(rows)])
        found += [far, lax.ppermute(far, "row", [(i, i ^ 1) for i in range(rows)])]
    return found


def gather_rows(pieces, rows):
    landed = lax.all_to_all(pieces, "col", split_axis=0, concat_axis=0, tiled=True)
    landed = landed.reshape((rows,) + pieces.shape[2:])
    landed = lax.all_to_all(landed, "row", split_axis=0, concat_axis=0, tiled=True)
    return lax.all_gather(landed, "col", axis=0, tiled=True)


def local(
    alignment,
    pair_state,
    alignment_factor_weight,
    outer_proj,
    outgoing_proj,
    outgoing_final,
    incoming_proj,
    incoming_final,
):
    seq = alignment.shape[0]
    row_tokens, col_tokens, channels = pair_state.shape
    hid_outer = alignment_factor_weight.shape[1] // 2
    hid = outgoing_final.shape[0]
    rows, cols = lax.axis_size("row"), lax.axis_size("col")
    count = rows * cols
    total = rows * seq
    per = LANES // hid_outer
    positions = row_tokens * col_tokens
    groups = positions // LANES
    both = ("row", "col")
    shape = jax.ShapeDtypeStruct

    row_source, col_source = call(
        factor_kernel,
        (
            shape((cols, rows // cols, seq // cols, row_tokens * hid_outer), BF16),
            shape((seq, col_tokens * hid_outer), BF16),
        ),
        [],
        alignment,
        alignment_factor_weight,
    )
    wide = call(
        functools.partial(widen_kernel, hid=hid_outer, scale=1.0 / total),
        shape((hid_outer // 2 * LANES, per // 2 * channels), BF16),
        [pltpu.VMEM(outer_proj.shape, F32)],
        outer_proj,
    )
    col_all = gather_blocks(col_source, rows)
    row_all = gather_rows(row_source, rows)

    state = shape((channels, positions), F32)
    wire = shape((count, 2 * hid // count * groups, LANES), BF16)
    turned = pltpu.VMEM((hid * groups, LANES), F32)
    pair, factors, gate = call(
        functools.partial(opm_kernel, hid=hid_outer, rows=rows, cols=cols),
        (state, wire, state),
        [
            pltpu.VMEM((total, row_tokens * hid_outer), BF16),
            pltpu.VMEM((col_tokens * hid_outer, total), BF16),
            pltpu.VMEM((positions * hid_outer * hid_outer // LANES, LANES), F32),
            pltpu.VMEM((positions * 2 // per, hid_outer // 2 * LANES), BF16),
            turned,
            turned,
        ],
        row_all,
        wide,
        near(pair_state),
        near(outgoing_proj),
        *col_all,
    )

    def mix(factors, outgoing):
        factors = lax.all_to_all(factors, both, split_axis=0, concat_axis=0, tiled=True)
        whole = (rows * row_tokens, cols * col_tokens)
        mixed = call(
            functools.partial(
                mix_kernel,
                rows=rows,
                cols=cols,
                row_tokens=row_tokens,
                col_tokens=col_tokens,
                outgoing=outgoing,
            ),
            shape((count, hid // count * groups, LANES), BF16),
            [pltpu.VMEM(whole, BF16)] * 2,
            factors,
        )
        return lax.all_to_all(mixed, both, split_axis=0, concat_axis=0, tiled=True)

    pair, factors, gate = call(
        finish_kernel,
        (state, wire, state),
        [turned, turned, turned],
        mix(factors, True),
        pair,
        gate,
        near(outgoing_final),
        near(incoming_proj),
    )
    return call(
        last_kernel,
        shape(pair_state.shape, F32),
        [turned],
        mix(factors, False),
        pair,
        gate,
        near(incoming_final),
        keep=False,
    )


def solution(mesh):
    return jax.shard_map(
        local,
        mesh=mesh,
        in_specs=(P("row", "col"), P("row", "col", None), P(), P(), P(), P(), P(), P()),
        out_specs=P("row", "col", None),
        check_vma=False,
    )
```
